128 devices in a mesh: node: 16 (over z, y), local: 8 (over x, core).
Axes of the slice: x: 4, y: 4, z: 4, core: 2. Of those that a mesh axis runs over, the one named last changes fastest.
Arguments:
- out_grad: bfloat16 [2048, 3584], P(('node', 'local')), may hold values from -6 to 6
- saved_input: bfloat16 [2048, 3584], P(('node', 'local')), may hold values from -6 to 6
- routes: int32 [2048, 8], P(('node', 'local')), may hold values from 0 to 127, as said below
- gate_int: int32 [2048, 8], P(('node', 'local')), may hold values from 4096 to 65535
- w_gate: bfloat16 [128, 3584, 1024], P(('node', 'local')), may hold values from -0.09375 to 0.09375
- w_up: bfloat16 [128, 3584, 1024], P(('node', 'local')), may hold values from -0.09375 to 0.09375
- w_down: bfloat16 [128, 1024, 3584], P(('node', 'local')), may hold values from -0.09375 to 0.09375
Outputs:
- input_grad: bfloat16 [2048, 3584], P(('node', 'local'))
- gate_grad: bfloat16 [2048, 8], P(('node', 'local'))
The draws below stay inside these ranges and needn't reach their ends.
Inputs may be any that keep to these rules, and one draw needn't show every extreme that they name: `routes`: each token names 8 different experts; picks 2 j and 2 j + 1 of a token lie in one node group (expert e is in group e // 8), and the four groups of a token differ. The 16 tokens of one device name one expert at most 2 times and one node group at most 8 times.
All inputs are finite; a program needn't handle non-finite values.
Results may differ from the reference program's by a relative error of at most 0.012.
Values may be sent and summed in bfloat16 or wider, within the bound.
A program may use at most 128 MiB of HBM per device.

```python
import jax
import jax.numpy as jnp
from jax import lax

D = 3584
F = 1024
TOPK = 8
TOK_DEV = 16
EXPERTS = 128
TOKENS = 2048
SLOT = 2
N_NODE = 16
N_LOCAL = 8


def draw_routes(key, part):
    device_total = TOKENS // TOK_DEV
    group_bias = jax.random.randint(jax.random.fold_in(key, 11), (N_NODE,), 0, 4)
    favoured = jax.random.randint(jax.random.fold_in(key, 12), (), 0, N_NODE)
    group_ids = jnp.arange(N_NODE, dtype=jnp.int32)
    group_bias = jnp.where(group_ids == favoured, 8, group_bias)
    half_tokens = TOK_DEV // 2
    cold_blocks = (N_NODE - 4) // 4
    pair_total = N_LOCAL // 2
    column = jnp.arange(4, dtype=jnp.int32)

    def one_device(device):
        device_key = jax.random.fold_in(key, 1000 + device)
        noise_draw = jax.random.randint(jax.random.fold_in(device_key, 1), (N_NODE,), 0, 16384)
        scores = group_bias * 1048576 + noise_draw * 64 + group_ids
        ranking = jnp.argsort(-scores).astype(jnp.int32)
        hot_groups = ranking[:4]
        cold_groups = ranking[4:]
        shuffle = jax.random.permutation(jax.random.fold_in(device_key, 2), N_LOCAL).astype(jnp.int32)
        token_rank = jax.random.permutation(jax.random.fold_in(device_key, 3), TOK_DEV).astype(jnp.int32)
        is_hot = token_rank < half_tokens
        cold_rank = jnp.maximum(token_rank - half_tokens, 0)
        cold_index = (cold_rank % cold_blocks)[:, None] * 4 + column[None, :]
        groups = jnp.where(is_hot[:, None], hot_groups[None, :], cold_groups[cold_index])
        base_rank = jnp.where(is_hot, token_rank, cold_rank // cold_blocks)
        pair_pick = (base_rank[:, None] + column[None, :]) % pair_total
        first_local = shuffle[2 * pair_pick]
        second_local = shuffle[2 * pair_pick + 1]
        experts = jnp.stack([groups * N_LOCAL + first_local, groups * N_LOCAL + second_local], axis=-1)
        return experts.reshape(TOK_DEV, TOPK).astype(jnp.int32)
    return jax.vmap(one_device)(jnp.arange(device_total, dtype=jnp.int32)).reshape(TOKENS, TOPK)


def place_ends(values, key, smallest, high):
    extent = values.shape
    place = [jax.random.randint(jax.random.fold_in(key, axis), (), 0, extent[axis]) for axis in range(len(extent))]
    values = values.at[tuple(place)].set(smallest)
    longest = extent.index(max(extent))
    place[longest] = (place[longest] + 1) % extent[longest]
    return values.at[tuple(place)].set(high)


def block_scale(own_key, shape, cuts, smallest, largest):
    def one(position, shards_of):
        heights = jax.random.uniform(jax.random.fold_in(jax.random.fold_in(own_key, 6), position), (shards_of,), jnp.float32, smallest / len(cuts), largest / len(cuts))
        return jnp.repeat(jnp.exp(heights), shape[position] // shards_of).reshape((-1,) + (1,) * (len(shape) - position - 1))

    gain = one(*cuts[0])
    for cut in cuts[1:]:
        gain = gain * one(*cut)
    return gain


def gaussian(own_key, extent, spread, most, split=(), kind=jnp.bfloat16):
    array = spread * jax.random.normal(own_key, extent, jnp.float32)
    if split:
        array = array * block_scale(own_key, extent, split, -0.22, 0.18)
    return jnp.clip(array, -most, most).astype(kind)


def setup_inputs(seed: int = 0) -> dict:
    streams_of = jax.random.split(jax.random.key(seed), 8)
    out_grad = gaussian(streams_of[0], (TOKENS, D), 1.0, 6.0, ((0, 128),))
    saved_input = gaussian(streams_of[1], (TOKENS, D), 1.0, 6.0, ((0, 128),))
    routes = draw_routes(jax.random.fold_in(streams_of[7], 71), 0)
    gate_int = place_ends(jax.random.randint(streams_of[3], (TOKENS, TOPK), 4096, 65536), jax.random.fold_in(streams_of[3], 1), 4096, 65535).astype(jnp.int32)
    w_gate = gaussian(streams_of[4], (EXPERTS, D, F), D ** -0.5, 0.09375, ((0, 128),))
    w_up = gaussian(streams_of[5], (EXPERTS, D, F), D ** -0.5, 0.09375, ((0, 128),))
    w_down = gaussian(streams_of[6], (EXPERTS, F, D), D ** -0.5, 0.09375, ((0, 128),))
    return {"out_grad": out_grad, "saved_input": saved_input, "routes": routes, "gate_int": gate_int, "w_gate": w_gate, "w_up": w_up, "w_down": w_down}


def expert_backward(input_rows, grad_rows, gate_proj, up_proj, down_proj):
    pre_gate = jnp.dot(input_rows, gate_proj, preferred_element_type=jnp.float32)
    pre_up = jnp.dot(input_rows, up_proj, preferred_element_type=jnp.float32)
    grad_hidden = jnp.dot(grad_rows, down_proj.T, preferred_element_type=jnp.float32)
    sigmoid = jax.nn.sigmoid(pre_gate)
    activated = pre_gate * sigmoid
    gate_score = jnp.sum(activated * pre_up * grad_hidden, axis=-1).astype(jnp.bfloat16)
    grad_gate = (grad_hidden * pre_up * sigmoid * (1.0 + pre_gate * (1.0 - sigmoid))).astype(jnp.bfloat16)
    grad_up = (grad_hidden * activated).astype(jnp.bfloat16)
    row_grad = jnp.dot(grad_gate, gate_proj.T, preferred_element_type=jnp.float32)
    row_grad = row_grad + jnp.dot(grad_up, up_proj.T, preferred_element_type=jnp.float32)
    return row_grad.astype(jnp.bfloat16), gate_score


def reference(out_grad, saved_input, routes, gate_int, w_gate, w_up, w_down):
    token_count = routes.shape[0]
    top_count = routes.shape[1]
    pair_total = token_count * top_count
    feature_width = out_grad.shape[1]
    capacity = N_NODE * N_LOCAL * SLOT
    flat_expert = routes.reshape(-1).astype(jnp.int32)
    order_picks = jnp.argsort(flat_expert, stable=True).astype(jnp.int32)
    sorted_expert = flat_expert[order_picks]
    expert_ids = jnp.arange(EXPERTS, dtype=jnp.int32)
    expert_start = jnp.searchsorted(sorted_expert, expert_ids).astype(jnp.int32)
    expert_count = jnp.sum((flat_expert[None, :] == expert_ids[:, None]).astype(jnp.int32), axis=1)
    gate_flat = gate_int.reshape(-1).astype(jnp.float32) * (1.0 / 65536.0)

    def one_expert(state_pair, expert):
        group_acc, score_acc = state_pair
        offsets = jnp.arange(capacity, dtype=jnp.int32)
        valid_rows = offsets < expert_count[expert]
        pick_index = order_picks[jnp.clip(expert_start[expert] + offsets, 0, pair_total - 1)]
        token_ids = pick_index // top_count
        zero_value = jnp.zeros((), out_grad.dtype)
        input_rows = jnp.where(valid_rows[:, None], saved_input[token_ids], zero_value)
        grad_rows = jnp.where(valid_rows[:, None], out_grad[token_ids], zero_value)
        row_grad, gate_score = expert_backward(input_rows, grad_rows, w_gate[expert], w_up[expert], w_down[expert])
        target = jnp.where(valid_rows, pick_index, pair_total)
        weight = gate_flat[pick_index]
        group_acc = group_acc.at[target // 2].add(row_grad.astype(jnp.float32) * weight[:, None], mode="drop")
        score_acc = score_acc.at[target].set(gate_score, mode="drop")
        return (group_acc, score_acc), None

    start_state = (jnp.zeros((pair_total // 2, feature_width), jnp.float32), jnp.zeros((pair_total,), jnp.bfloat16))
    final_state, unused = lax.scan(one_expert, start_state, expert_ids)
    group_acc, score_acc = final_state
    group_grad = group_acc.astype(jnp.bfloat16).reshape(token_count, top_count // 2, feature_width)
    input_grad = jnp.sum(group_grad.astype(jnp.float32), axis=1).astype(jnp.bfloat16)
    gate_grad = score_acc.reshape(token_count, top_count)
    return input_grad, gate_grad
```

```python
import functools

import jax
import jax.numpy as jnp
from jax import lax
from jax.experimental import pallas as pl
from jax.experimental.pallas import tpu as pltpu
from jax.sharding import PartitionSpec as P

MESH = pl.DeviceIdType.MESH
BF = jnp.bfloat16
F32 = jnp.float32

ORDERS = (("x", "y", "z"), ("y", "z", "x"), ("z", "x", "y"))
WIDTHS = (1152, 1152, 1280)
OFFS = (0, 1152, 2304)
BACK_W = (512, 640, 640)
BACK_OFF = (0, 512, 1152)
BW = 640
STRIDE = {"z": 32, "y": 8, "x": 2}
SPLIT = {"z": 64, "y": 16, "x": 4}
NT = (((1,), (1,)), ((), ()))
TN = (((0,), (0,)), ((), ()))


def coords():
    node = lax.axis_index("node")
    local = lax.axis_index("local")
    return {"z": node // 4, "y": node % 4, "x": local // 2}, local % 2


def native_row(row, order):
    value = {a: (row // SPLIT[a]) % 4 for a in "xyz"}
    a1, a2, a3 = order
    return value[a3] * 64 + value[a2] * 16 + value[a1] * 4 + row % 4


def dot(a, b):
    return jnp.dot(a, b, preferred_element_type=F32)


def kernel(
    og, si, routes, gate_int, wg_hbm, wu_hbm, wd_hbm, out, gout,
    b0, b1, b2, mown, mrecv, ms, smat, kmask, sb0, sb1, sb2, gb, gr, xx, r1, r2,
    wg, wu, wd, gg, gu, score, ys, yr, zs, zr, vs, vr, fin, outs,
    wsem, s0, e0, sm1, em1, s1, e1, sm2, em2, s2, e2, s3, e3, sg, eg, t3, f3, t2, f2, t1, f1, t0, f0,
):
    pos, core = coords()
    bb, sb = (b0, b1, b2), (sb0, sb1, sb2)

    def at(axis, d, cc):
        p = dict(pos)
        p[axis] = (pos[axis] + d) % 4
        return (p["z"] * 4 + p["y"], p["x"] * 2 + (core + cc) % 2)

    def remote(src, dst, send, recv, axis, d, cc):
        return pltpu.make_async_remote_copy(
            src_ref=src, dst_ref=dst, send_sem=send, recv_sem=recv, device_id=at(axis, d, cc), device_id_type=MESH
        )

    loads = [
        pltpu.make_async_copy(hbm.at[0], vmem, wsem.at[i])
        for i, (hbm, vmem) in enumerate(((wg_hbm, wg), (wu_hbm, wu), (wd_hbm, wd)))
    ]
    for copy in loads:
        copy.start()

    barrier = pltpu.get_barrier_semaphore()
    partners = [("x", 0, 1)] + [(a, d, cc) for a in "xyz" for d in (1, 2, 3) for cc in (0, 1)]
    for a, d, cc in partners:
        pl.semaphore_signal(barrier, inc=1, device_id=at(a, d, cc), device_id_type=MESH)

    gate_i = gate_int[...]
    table = jnp.concatenate([routes[...], gate_i // 256, gate_i % 256], axis=1).astype(F32).astype(BF)
    token = lax.broadcasted_iota(jnp.int32, (16, 128), 0)
    lane = lax.broadcasted_iota(jnp.int32, (16, 128), 1)
    for q, (a1, a2, a3) in enumerate(ORDERS):
        place = (lane == pos[a1] * 32 + core * 16 + token).astype(F32).astype(BF)
        laid = lax.dot_general(table, place, TN, preferred_element_type=F32)
        mown[q, 0:8, :] = laid[0:8]
        mown[q, 8:16, :] = laid[8:16] * 256.0 + laid[16:24]

    pl.semaphore_wait(barrier, len(partners))

    def split(q, mine, other):
        a1, a2, a3 = ORDERS[q]
        rows = pl.ds(pl.multiple_of(pos[a1] * 32 + core * 16, 16), 16)
        cols = pl.ds(OFFS[q], WIDTHS[q])
        dst = bb[q].at[pos[a2], rows, :]
        return (
            pltpu.make_async_copy(mine.at[:, cols], dst, s0.at[q, 0]),
            remote(other.at[:, cols], dst, s0.at[q, 1], e0.at[q], "x", 0, 1),
        )

    for which, (mine, other) in enumerate(((og, si), (si, og))):

        @pl.when(core == which)
        def _(mine=mine, other=other):
            for q in range(3):
                for copy in split(q, mine, other):
                    copy.start()

    hops = [(d, cc) for d in range(4) for cc in range(2) if (d, cc) != (0, 0)]
    metas = {}
    for q, (a1, a2, a3) in enumerate(ORDERS):
        for d, cc in hops:
            copy = remote(
                mown.at[q], mrecv.at[q, pos[a1] * 2 + core], sm1.at[q, d, cc], em1.at[q, d, cc], a1, d, cc
            )
            copy.start()
            metas[q, d, cc] = copy
        mrecv[q, pos[a1] * 2 + core] = mown[q]

    firsts = {}
    for q, (a1, a2, a3) in enumerate(ORDERS):
        for copy in split(q, og, si):
            copy.wait()
        mine = bb[q].at[pos[a2], pl.ds(pl.multiple_of(pos[a1] * 32, 32), 32), :]
        for d in (2, 1, 3):
            firsts[q, d] = remote(mine, mine, s1.at[q, d], e1.at[q, d], a1, d, 0)
            firsts[q, d].start()

    meta2 = {}
    for q, (a1, a2, a3) in enumerate(ORDERS):
        for d, cc in hops:
            metas[q, d, cc].wait()
        ms[q, pos[a2]] = jnp.sum(mrecv[q], axis=0)
        for d in (1, 2, 3):
            meta2[q, d] = remote(ms.at[q, pos[a2]], ms.at[q, pos[a2]], sm2.at[q, d], em2.at[q, d], a2, d, 0)
            meta2[q, d].start()

    seconds = {}
    for q, (a1, a2, a3) in enumerate(ORDERS):
        for d in (1, 2, 3):
            firsts[q, d].wait()
        for d in (2, 1, 3):
            seconds[q, d] = remote(bb[q].at[pos[a2]], bb[q].at[pos[a2]], s2.at[q, d], e2.at[q, d], a2, d, 0)
            seconds[q, d].start()

    up = lax.broadcasted_iota(jnp.int32, (128, 128), 0)
    across = lax.broadcasted_iota(jnp.int32, (128, 128), 1)
    earlier = ((up < across) & (up // 16 == across // 16)).astype(F32).astype(BF)
    lanes3 = lax.broadcasted_iota(jnp.int32, (8, 16, 128), 2)
    slots3 = lax.broadcasted_iota(jnp.int32, (8, 16, 128), 1).astype(F32)
    picks3 = lax.broadcasted_iota(jnp.int32, (8, 8, 128), 1).astype(F32)
    expert3 = lax.broadcasted_iota(jnp.int32, (8, 8, 128), 0)
    pair = ((lax.broadcasted_iota(jnp.int32, (8, 128), 1) // 16) * 2).astype(F32)

    def tables(q, block):
        a1, a2, a3 = ORDERS[q]
        base = pos[a1] * STRIDE[a1] + pos[a2] * STRIDE[a2]
        expert = ((expert3 // 2) * STRIDE[a3] + expert3 % 2 + base).astype(F32)
        meta = ms[q, block]
        hit = jnp.where(meta[0:8][None] == expert, 1.0, 0.0)
        named = jnp.sum(hit, axis=1)
        rank = dot(named.astype(BF), earlier)
        code = jnp.where(named > 0.5, pair + rank, -1.0)
        chosen = jnp.where(code[:, None, :] == slots3, 1.0, 0.0)
        smat[q, block] = chosen.reshape(128, 128).astype(BF)
        if q == 0:
            rows = pl.ds(pl.multiple_of(block * 16, 16), 16)
            gate = jnp.sum(hit * meta[8:16][None], axis=1)
            gate = jnp.sum(chosen * gate[:, None, :], axis=2, keepdims=True)
            gb[:, rows, :] = jnp.broadcast_to(gate * (1.0 / 65536.0), (8, 16, 128))
            pick = jnp.sum(hit * picks3, axis=1)
            pick = jnp.sum(chosen * pick[:, None, :], axis=2, keepdims=True)
            kmask[block] = jnp.where(lanes3.astype(F32) == pick, 1.0, 0.0).reshape(128, 128).astype(BF)

    def pack(q, block):
        rows = pl.ds(pl.multiple_of(block * 16, 16), 16)
        taken = dot(smat[q, block], bb[q][block])
        sb[q][:, rows, :] = taken.astype(BF).reshape(8, 16, WIDTHS[q])

    for q, (a1, a2, a3) in enumerate(ORDERS):
        for d in (1, 2, 3):
            meta2[q, d].wait()

        def each(block, carry, q=q):
            tables(q, block)
            return carry

        lax.fori_loop(0, 4, each, 0)

    gates = {}
    gmine = gr.at[pl.ds(pl.multiple_of(pos["z"] * 64, 64), 64), :]
    for d in range(4):
        src = gb.at[((pos["z"] + d) % 4) * 2 + core]
        gates[d] = pltpu.make_async_copy(src, gmine, sg.at[d]) if d == 0 else remote(
            src, gmine, sg.at[d], eg.at[d], "z", d, 0
        )
        gates[d].start()

    thirds = {}
    for q, (a1, a2, a3) in enumerate(ORDERS):
        pack(q, pos[a2])
        for d in (1, 3, 2):
            seconds[q, d].wait()
        for d in (1, 2, 3):
            pack(q, (pos[a2] + d) % 4)
        rows = pl.ds(pl.multiple_of(pos[a3] * 64, 64), 64)
        land = xx.at[core, rows, pl.ds(0, WIDTHS[0])] if q == 0 else (r1, r2)[q - 1].at[core, rows, :]
        for d in (2, 1, 3, 0):
            for cc in (1, 0):
                src = sb[q].at[((pos[a3] + d) % 4) * 2 + (core + cc) % 2]
                if (d, cc) == (0, 0):
                    copy = pltpu.make_async_copy(src, land, s3.at[q, 0, 0])
                else:
                    copy = remote(src, land, s3.at[q, d, cc], e3.at[q, d, cc], a3, d, cc)
                copy.start()
                thirds[q, d, cc] = copy

    iota_r = lax.broadcasted_iota(jnp.int32, (256, 256), 0)
    iota_c = lax.broadcasted_iota(jnp.int32, (256, 256), 1)
    for q in range(3):
        for d in range(4):
            for cc in (0, 1):
                thirds[q, d, cc].wait()
        if q:
            perm = (native_row(iota_r, ORDERS[q]) == iota_c).astype(F32).astype(BF)
            for kind in range(2):
                xx[kind, :, OFFS[q] : OFFS[q] + WIDTHS[q]] = dot(perm, (r1, r2)[q - 1][kind]).astype(BF)
    for d in range(4):
        gates[d].wait()
    for copy in loads:
        copy.wait()

    score[...] = jnp.zeros_like(score)

    def hidden(n, carry):
        at_n = pl.ds(pl.multiple_of(n * 256, 256), 256)
        pre_gate = dot(xx[1], wg[:, at_n])
        pre_up = dot(xx[1], wu[:, at_n])
        grad_hidden = lax.dot_general(xx[0], wd[at_n, :], NT, preferred_element_type=F32)
        sig = jax.nn.sigmoid(pre_gate)
        act = pre_gate * sig
        grad_up = grad_hidden * act
        part = grad_up * pre_up
        score[...] += part[:, 0:128] + part[:, 128:256]
        gu[:, at_n] = grad_up.astype(BF)
        gg[:, at_n] = (grad_hidden * pre_up * sig * (1.0 + pre_gate * (1.0 - sig))).astype(BF)
        return carry

    lax.fori_loop(0, 4, hidden, 0)

    backs = {}
    for q, (a1, a2, a3) in enumerate(ORDERS):
        w = BACK_W[q]
        for half in range(2):
            cols = pl.ds(half * 1792 + BACK_OFF[q], w)
            rows = lax.dot_general(gg[...], wg[cols, :], NT, preferred_element_type=F32)
            rows = rows + lax.dot_general(gu[...], wu[cols, :], NT, preferred_element_type=F32)
            rows = (rows * gr[:, 0:1]).astype(BF)
            if q:
                back = (native_row(iota_c, ORDERS[q]) == iota_r).astype(F32).astype(BF)
                rows = dot(back, rows).astype(BF)
            else:
                total = jnp.sum(score[...], axis=1, keepdims=True)
                ys[q, half, :, w:BW] = jnp.broadcast_to(total, (256, 128)).astype(BF)
            ys[q, half, :, 0:w] = rows
        mine = yr.at[q, pos[a3] * 2 + core]
        for d in (2, 1, 3, 0):
            for cc in (1, 0):
                there = pl.ds(pl.multiple_of(((pos[a3] + d) % 4) * 64, 64), 64)
                src = ys.at[q, (core + cc) % 2, there, :]
                if (d, cc) == (0, 0):
                    copy = pltpu.make_async_copy(src, mine, t3.at[q, 0, 0])
                else:
                    copy = remote(src, mine, t3.at[q, d, cc], f3.at[q, d, cc], a3, d, cc)
                copy.start()
                backs[q, d, cc] = copy

    sums = {}
    for q, (a1, a2, a3) in enumerate(ORDERS):
        for d in range(4):
            for cc in (0, 1):
                backs[q, d, cc].wait()
        for d in (2, 1, 3, 0):
            block = (pos[a2] + d) % 4
            rows = pl.ds(pl.multiple_of(block * 16, 16), 16)
            got = yr[q, :, rows, :].reshape(128, BW)
            if q == 0:
                got = jnp.concatenate([got[:, 0:512], got[:, 512:640] * kmask[block]], axis=1)
            total = lax.dot_general(smat[q, block], got, TN, preferred_element_type=F32).astype(BF)
            if d == 0:
                zr[q, pos[a2]] = total
            else:
                zs[q, block] = total
                sums[q, d] = remote(zs.at[q, block], zr.at[q, pos[a2]], t2.at[q, d], f2.at[q, d], a2, d, 0)
                sums[q, d].start()

    lasts = {}
    for q, (a1, a2, a3) in enumerate(ORDERS):
        for d in (1, 3, 2):
            sums[q, d].wait()
        total = jnp.zeros((128, BW), F32)
        for s in range(4):
            total = total + zr[q, s].astype(F32)
        vs[q] = total.astype(BF)
        for d in (2, 1, 3):
            there = pl.ds(pl.multiple_of(((pos[a1] + d) % 4) * 32, 32), 32)
            lasts[q, d] = remote(vs.at[q, there, :], vr.at[q, pos[a1]], t1.at[q, d], f1.at[q, d], a1, d, 0)
            lasts[q, d].start()
        vr[q, pos[a1]] = vs[q, pl.ds(pl.multiple_of(pos[a1] * 32, 32), 32), :]

    for q, (a1, a2, a3) in enumerate(ORDERS):
        for d in (1, 3, 2):
            lasts[q, d].wait()
        total = jnp.zeros((32, BW), F32)
        for s in range(4):
            total = total + vr[q, s].astype(F32)
        fin[:, q * BW : (q + 1) * BW] = total.astype(BF)

    own = pl.ds(pl.multiple_of(core * 16, 16), 16)
    sibling = pl.ds(pl.multiple_of((1 - core) * 16, 16), 16)
    copy = remote(fin.at[sibling, :], outs.at[core], t0.at[0], f0.at[0], "x", 0, 1)
    copy.start()
    outs[core] = fin[own, :]
    gout[...] = fin[own, 512:520]
    copy.wait()
    for half in range(2):
        for q in range(3):
            start = half * 1792 + BACK_OFF[q]
            out[:, start : start + BACK_W[q]] = outs[half, :, q * BW : q * BW + BACK_W[q]]


def shards(out_grad, saved_input, routes, gate_int, w_gate, w_up, w_down):
    vmem = pl.BlockSpec(memory_space=pltpu.VMEM)
    hbm = pl.BlockSpec(memory_space=pl.ANY)
    sem = pltpu.SemaphoreType.DMA
    scratch = (
        [pltpu.VMEM((4, 128, w), BF) for w in WIDTHS]
        + [
            pltpu.VMEM((3, 16, 128), F32),
            pltpu.VMEM((3, 8, 16, 128), F32),
            pltpu.VMEM((3, 4, 16, 128), F32),
            pltpu.VMEM((3, 4, 128, 128), BF),
            pltpu.VMEM((4, 128, 128), BF),
        ]
        + [pltpu.VMEM((8, 64, w), BF) for w in WIDTHS]
        + [
            pltpu.VMEM((8, 64, 128), F32),
            pltpu.VMEM((256, 128), F32),
            pltpu.VMEM((2, 256, 3584), BF),
            pltpu.VMEM((2, 256, WIDTHS[1]), BF),
            pltpu.VMEM((2, 256, WIDTHS[2]), BF),
            pltpu.VMEM((3584, 1024), BF),
            pltpu.VMEM((3584, 1024), BF),
            pltpu.VMEM((1024, 3584), BF),
            pltpu.VMEM((256, 1024), BF),
            pltpu.VMEM((256, 1024), BF),
            pltpu.VMEM((256, 128), F32),
            pltpu.VMEM((3, 2, 256, BW), BF),
            pltpu.VMEM((3, 8, 64, BW), BF),
            pltpu.VMEM((3, 4, 128, BW), BF),
            pltpu.VMEM((3, 4, 128, BW), BF),
            pltpu.VMEM((3, 128, BW), BF),
            pltpu.VMEM((3, 4, 32, BW), BF),
            pltpu.VMEM((32, 3 * BW), BF),
            pltpu.VMEM((2, 16, 3 * BW), BF),
        ]
        + [
            sem((3,)),
            sem((3, 2)), sem((3,)),
            sem((3, 4, 2)), sem((3, 4, 2)),
            sem((3, 4)), sem((3, 4)),
            sem((3, 4)), sem((3, 4)),
            sem((3, 4)), sem((3, 4)),
            sem((3, 4, 2)), sem((3, 4, 2)),
            sem((4,)), sem((4,)),
            sem((3, 4, 2)), sem((3, 4, 2)),
            sem((3, 4)), sem((3, 4)),
            sem((3, 4)), sem((3, 4)),
            sem((1,)), sem((1,)),
        ]
    )
    return tuple(
        pl.pallas_call(
            kernel,
            out_shape=(
                jax.ShapeDtypeStruct(out_grad.shape, BF),
                jax.ShapeDtypeStruct(routes.shape, BF),
            ),
            in_specs=[hbm, hbm, vmem, vmem, hbm, hbm, hbm],
            out_specs=(vmem, vmem),
            scratch_shapes=scratch,
            compiler_params=pltpu.CompilerParams(
                collective_id=0, has_side_effects=True, vmem_limit_bytes=64 * 2**20 - 65536
            ),
        )(out_grad, saved_input, routes, gate_int, w_gate, w_up, w_down)
    )


def solution(mesh):
    rows = P(("node", "local"), None)
    experts = P(("node", "local"), None, None)
    return jax.shard_map(
        shards,
        mesh=mesh,
        in_specs=(rows, rows, rows, rows, experts, experts, experts),
        out_specs=(rows, rows),
        check_vma=False,
    )
```

```python
import functools

import jax
import jax.numpy as jnp
from jax import lax
from jax.experimental import pallas as pl
from jax.experimental.pallas import tpu as pltpu
from jax.sharding import PartitionSpec as P

MESH = pl.DeviceIdType.MESH
BF = jnp.bfloat16
F32 = jnp.float32

ORDERS = (("x", "y", "z"), ("y", "z", "x"), ("z", "x", "y"))
HALF = 1792
WIDTHS = (640, 640, 512)
OFFS = (0, 640, 1280)
UNITS = ((0, 0), (0, 1), (0, 2), (1, 0), (1, 1), (1, 2))
BACK_W = {(0, 0): 256, (0, 1): 256, (0, 2): 256, (1, 0): 256, (1, 1): 384, (1, 2): 384}
BACK_OFF = {(0, 0): 0, (0, 1): 512, (0, 2): 1024, (1, 0): 1536, (1, 1): 2048, (1, 2): 2816}
BW = (256, 384)
FIN = {(0, 0): 0, (0, 1): 256, (0, 2): 512, (1, 0): 768, (1, 1): 1152, (1, 2): 1536}
FIN_W = 1920
STRIDE = {"z": 32, "y": 8, "x": 2}
SPLIT = {"z": 64, "y": 16, "x": 4}
NT = (((1,), (1,)), ((), ()))
TN = (((0,), (0,)), ((), ()))


def coords():
    node = lax.axis_index("node")
    local = lax.axis_index("local")
    return {"z": node // 4, "y": node % 4, "x": local // 2}, local % 2


def native_row(row, order):
    value = {a: (row // SPLIT[a]) % 4 for a in "xyz"}
    a1, a2, a3 = order
    return value[a3] * 64 + value[a2] * 16 + value[a1] * 4 + row % 4


def dot(a, b):
    return jnp.dot(a, b, preferred_element_type=F32)


def kernel(
    og, si, routes, gate_int, wg_hbm, wu_hbm, wd_hbm, out, gout,
    b0, b1, b2, mown, mrecv, msum, ms, smat, kmask, sb0, sb1, sb2, gb, gr, xx, r1, r2,
    wg, wu, wd, pre, gg, gu, score, ysa, ysb, yra, yrb, zsa, zsb, zra, zrb, vsa, vsb, vra, vrb, fin, outs,
    wsem, s0, e0, sm1, em1, s1, e1, sm2, em2, s2, e2, s3, e3, sg, eg, t3, f3, t2, f2, t1, f1, t0, f0,
):
    pos, core = coords()
    bb, sb = (b0, b1, b2), (sb0, sb1, sb2)
    ys, yr, zs, zr, vs, vr = (ysa, ysb), (yra, yrb), (zsa, zsb), (zra, zrb), (vsa, vsb), (vra, vrb)
    KINDS = (1, 0)

    def at(axis, d, cc):
        p = dict(pos)
        p[axis] = (pos[axis] + d) % 4
        return (p["z"] * 4 + p["y"], p["x"] * 2 + (core + cc) % 2)

    def remote(src, dst, send, recv, axis, d, cc):
        return pltpu.make_async_remote_copy(
            src_ref=src, dst_ref=dst, send_sem=send, recv_sem=recv, device_id=at(axis, d, cc), device_id_type=MESH
        )

    def block(index, size):
        return pl.ds(pl.multiple_of(index * size, size), size)

    loads = [
        pltpu.make_async_copy(hbm.at[0], vmem, wsem.at[i])
        for i, (hbm, vmem) in enumerate(((wg_hbm, wg), (wu_hbm, wu), (wd_hbm, wd)))
    ]
    for copy in loads:
        copy.start()

    barrier = pltpu.get_barrier_semaphore()
    partners = [("x", 0, 1)] + [(a, d, cc) for a in "xyz" for d in (1, 2, 3) for cc in (0, 1)]
    for a, d, cc in partners:
        pl.semaphore_signal(barrier, inc=1, device_id=at(a, d, cc), device_id_type=MESH)

    gate_i = gate_int[...]
    table = jnp.concatenate([routes[...], gate_i // 256, gate_i % 256], axis=0).astype(F32).astype(BF)
    token = lax.broadcasted_iota(jnp.int32, (16, 128), 0)
    lane = lax.broadcasted_iota(jnp.int32, (16, 128), 1)
    for q, (a1, a2, a3) in enumerate(ORDERS):
        place = (lane == pos[a1] * 32 + core * 16 + token).astype(F32).astype(BF)
        laid = dot(table, place)
        mown[q, 0:8, :] = laid[0:8]
        mown[q, 8:16, :] = laid[8:16] * 256.0 + laid[16:24]

    pl.semaphore_wait(barrier, len(partners))

    splits = {}
    for k in KINDS:
        source = (og, si)[k]
        for q, (a1, a2, a3) in enumerate(ORDERS):
            dst = bb[q].at[k, pos[a2], block(pos[a1] * 2 + core, 16), :]
            mine = pl.ds(pl.multiple_of(core * HALF + OFFS[q], 128), WIDTHS[q])
            other = pl.ds(pl.multiple_of((1 - core) * HALF + OFFS[q], 128), WIDTHS[q])
            splits[k, q, 1] = remote(source.at[:, other], dst, s0.at[k, q, 1], e0.at[k, q], "x", 0, 1)
            splits[k, q, 0] = pltpu.make_async_copy(source.at[:, mine], dst, s0.at[k, q, 0])
            splits[k, q, 1].start()
            splits[k, q, 0].start()

    hops = [(d, cc) for d in range(4) for cc in range(2) if (d, cc) != (0, 0)]
    metas = {}
    for q, (a1, a2, a3) in enumerate(ORDERS):
        for d, cc in hops:
            copy = remote(mown.at[q], mrecv.at[q, pos[a1] * 2 + core], sm1.at[q, d, cc], em1.at[q, d, cc], a1, d, cc)
            copy.start()
            metas[q, d, cc] = copy
        mrecv[q, pos[a1] * 2 + core] = mown[q]

    firsts = {}
    for k in KINDS:
        for q, (a1, a2, a3) in enumerate(ORDERS):
            splits[k, q, 0].wait()
            splits[k, q, 1].wait()
            mine = bb[q].at[k, pos[a2], block(pos[a1], 32), :]
            for d in (2, 1, 3):
                firsts[k, q, d] = remote(mine, mine, s1.at[k, q, d], e1.at[k, q, d], a1, d, 0)
                firsts[k, q, d].start()

    meta2 = {}
    for q, (a1, a2, a3) in enumerate(ORDERS):
        for d, cc in hops:
            metas[q, d, cc].wait()
        total = jnp.sum(mrecv[q], axis=0)
        msum[q] = total
        ms[q, pos[a2]] = total
        for d in (1, 2, 3):
            meta2[q, d] = remote(msum.at[q], ms.at[q, pos[a2]], sm2.at[q, d], em2.at[q, d], a2, d, 0)
            meta2[q, d].start()

    seconds = {}
    for k in KINDS:
        for q, (a1, a2, a3) in enumerate(ORDERS):
            for d in (1, 2, 3):
                firsts[k, q, d].wait()
            mine = bb[q].at[k, pos[a2]]
            for d in (1, 3):
                seconds[k, q, d] = remote(mine, mine, s2.at[k, q, d], e2.at[k, q, d], a2, d, 0)
                seconds[k, q, d].start()
    for k in KINDS:
        for q, (a1, a2, a3) in enumerate(ORDERS):
            for d, part in ((1, 0), (3, 1)):
                seconds[k, q, d].wait()
                held = bb[q].at[k, (pos[a2] - d) % 4, pl.ds(part * 64, 64), :]
                copy = remote(held, held, s2.at[k, q, d - 1], e2.at[k, q, d - 1], a2, d, 0)
                copy.start()
                seconds[k, q, d - 1] = copy

    up = lax.broadcasted_iota(jnp.int32, (256, 256), 0)
    across = lax.broadcasted_iota(jnp.int32, (256, 256), 1)
    earlier = ((up < across) & (up // 16 == across // 16)).astype(F32).astype(BF)
    lanes3 = lax.broadcasted_iota(jnp.int32, (8, 32, 128), 2).astype(F32)
    slots3 = lax.broadcasted_iota(jnp.int32, (8, 32, 256), 1).astype(F32)
    picks3 = lax.broadcasted_iota(jnp.int32, (8, 8, 256), 1).astype(F32)
    expert3 = lax.broadcasted_iota(jnp.int32, (8, 8, 256), 0)
    pair = ((lax.broadcasted_iota(jnp.int32, (8, 256), 1) // 16) * 2).astype(F32)

    def tables(q, p):
        a1, a2, a3 = ORDERS[q]
        base = pos[a1] * STRIDE[a1] + pos[a2] * STRIDE[a2]
        expert = ((expert3 // 2) * STRIDE[a3] + expert3 % 2 + base).astype(F32)
        meta = jnp.concatenate([ms[q, 2 * p], ms[q, 2 * p + 1]], axis=1)
        hit = jnp.where(meta[0:8][None] == expert, 1.0, 0.0)
        named = jnp.sum(hit, axis=1)
        rank = dot(named.astype(BF), earlier)
        code = jnp.where(named > 0.5, pair + rank, -1.0)
        chosen = jnp.where(code[:, None, :] == slots3, 1.0, 0.0)
        smat[q, p] = chosen.reshape(256, 256).astype(BF)
        if q == 0:
            gate = jnp.sum(hit * meta[8:16][None], axis=1)
            gate = jnp.sum(chosen * gate[:, None, :], axis=2, keepdims=True)
            gb[:, p * 32 : p * 32 + 32, :] = jnp.broadcast_to(gate * (1.0 / 65536.0), (8, 32, 128))
            pick = jnp.sum(hit * picks3, axis=1)
            pick = jnp.sum(chosen * pick[:, None, :], axis=2, keepdims=True)
            kmask[p] = jnp.where(lanes3 == pick, 1.0, 0.0).reshape(256, 128).astype(BF)

    gates = {}
    for q, (a1, a2, a3) in enumerate(ORDERS):
        for d in (1, 2, 3):
            meta2[q, d].wait()
        for p in range(2):
            tables(q, p)
        if q == 0:
            gmine = gr.at[block(pos["z"], 64), :]
            for d in range(4):
                src = gb.at[((pos["z"] + d) % 4) * 2 + core]
                if d == 0:
                    gates[d] = pltpu.make_async_copy(src, gmine, sg.at[d])
                else:
                    gates[d] = remote(src, gmine, sg.at[d], eg.at[d], "z", d, 0)
                gates[d].start()

    thirds = {}
    for k in KINDS:
        for q, (a1, a2, a3) in enumerate(ORDERS):
            for d in (0, 2):
                seconds[k, q, d].wait()
            for p in range(2):
                rows = dot(smat[q, p], bb[q][k, 2 * p : 2 * p + 2].reshape(256, WIDTHS[q]))
                sb[q][k, :, p * 32 : p * 32 + 32, :] = rows.astype(BF).reshape(8, 32, WIDTHS[q])
            there = block(pos[a3], 64)
            if q == 0:
                land = xx.at[k, there, pl.ds(pl.multiple_of(core * HALF, 128), WIDTHS[0])]
            else:
                land = (r1, r2)[q - 1].at[k, core, there, :]
            for d in (2, 1, 3, 0):
                for cc in (1, 0):
                    src = sb[q].at[k, ((pos[a3] + d) % 4) * 2 + (core + cc) % 2]
                    if (d, cc) == (0, 0):
                        copy = pltpu.make_async_copy(src, land, s3.at[k, q, 0, 0])
                    else:
                        copy = remote(src, land, s3.at[k, q, d, cc], e3.at[k, q, d, cc], a3, d, cc)
                    copy.start()
                    thirds[k, q, d, cc] = copy

    iota_r = lax.broadcasted_iota(jnp.int32, (256, 256), 0)
    iota_c = lax.broadcasted_iota(jnp.int32, (256, 256), 1)

    def arrive(k):
        for q in range(3):
            for d in range(4):
                for cc in (0, 1):
                    thirds[k, q, d, cc].wait()
            if q:
                perm = (native_row(iota_r, ORDERS[q]) == iota_c).astype(F32).astype(BF)
                for half in range(2):
                    start = half * HALF + OFFS[q]
                    rows = dot(perm, (r1, r2)[q - 1][k, half])
                    xx[k, :, start : start + WIDTHS[q]] = rows.astype(BF)

    arrive(1)
    for copy in loads:
        copy.wait()

    def forward(n, carry):
        at_n = block(n, 512)
        pre[0, :, at_n] = dot(xx[1], wg[:, at_n])
        pre[1, :, at_n] = dot(xx[1], wu[:, at_n])
        return carry

    lax.fori_loop(0, 2, forward, 0)
    arrive(0)
    score[...] = jnp.zeros_like(score)

    def backward(n, carry):
        at_n = block(n, 512)
        grad_hidden = lax.dot_general(xx[0], wd[at_n, :], NT, preferred_element_type=F32)
        pre_gate = pre[0, :, at_n]
        pre_up = pre[1, :, at_n]
        sig = jax.nn.sigmoid(pre_gate)
        act = pre_gate * sig
        grad_up = grad_hidden * act
        part = grad_up * pre_up
        score[...] += (part[:, 0:128] + part[:, 128:256]) + (part[:, 256:384] + part[:, 384:512])
        gu[:, at_n] = grad_up.astype(BF)
        gg[:, at_n] = (grad_hidden * pre_up * sig * (1.0 + pre_gate * (1.0 - sig))).astype(BF)
        return carry

    lax.fori_loop(0, 2, backward, 0)
    for d in range(4):
        gates[d].wait()

    backs = {}

    def expert_rows(t, q):
        a1, a2, a3 = ORDERS[q]
        w = BACK_W[t, q]
        cols = pl.ds(BACK_OFF[t, q], 2 * w)
        rows = lax.dot_general(gg[...], wg[cols, :], NT, preferred_element_type=F32)
        rows = rows + lax.dot_general(gu[...], wu[cols, :], NT, preferred_element_type=F32)
        rows = (rows * gr[:, 0:1]).astype(BF)
        if q:
            back = (native_row(iota_c, ORDERS[q]) == iota_r).astype(F32).astype(BF)
            rows = dot(back, rows).astype(BF)
        for half in range(2):
            ys[t][q, half, :, 0:w] = rows[:, half * w : (half + 1) * w]
            if w < BW[t]:
                total = jnp.sum(score[...], axis=1, keepdims=True)
                ys[t][q, half, :, w : BW[t]] = jnp.broadcast_to(total, (256, 128)).astype(BF)
        mine = yr[t].at[q, pos[a3] * 2 + core]
        for d in (2, 1, 3, 0):
            for cc in (1, 0):
                src = ys[t].at[q, (core + cc) % 2, block((pos[a3] + d) % 4, 64), :]
                if (d, cc) == (0, 0):
                    copy = pltpu.make_async_copy(src, mine, t3.at[t, q, 0, 0])
                else:
                    copy = remote(src, mine, t3.at[t, q, d, cc], f3.at[t, q, d, cc], a3, d, cc)
                copy.start()
                backs[t, q, d, cc] = copy

    sums = {}

    def combine(t, q):
        a1, a2, a3 = ORDERS[q]
        for d in range(4):
            for cc in (0, 1):
                backs[t, q, d, cc].wait()
        for p in range(2):
            got = yr[t][q, :, p * 32 : p * 32 + 32, :].reshape(256, BW[t])
            if BACK_W[t, q] < BW[t]:
                got = jnp.concatenate([got[:, 0:256], got[:, 256:384] * kmask[p]], axis=1)
            total = lax.dot_general(smat[q, p], got, TN, preferred_element_type=F32).astype(BF)
            zs[t][q, 2 * p : 2 * p + 2] = total.reshape(2, 128, BW[t])
        for d in (2, 1, 3, 0):
            src, dst = zs[t].at[q, (pos[a2] + d) % 4], zr[t].at[q, pos[a2]]
            if d == 0:
                copy = pltpu.make_async_copy(src, dst, t2.at[t, q, d])
            else:
                copy = remote(src, dst, t2.at[t, q, d], f2.at[t, q, d], a2, d, 0)
            copy.start()
            sums[t, q, d] = copy

    lasts = {}

    def narrow(t, q):
        a1, a2, a3 = ORDERS[q]
        for d in (0, 1, 3, 2):
            sums[t, q, d].wait()
        total = jnp.zeros((128, BW[t]), F32)
        for s in range(4):
            total = total + zr[t][q, s].astype(F32)
        vs[t][q] = total.astype(BF)
        for d in (2, 1, 3, 0):
            src, dst = vs[t].at[q, block((pos[a1] + d) % 4, 32), :], vr[t].at[q, pos[a1]]
            if d == 0:
                copy = pltpu.make_async_copy(src, dst, t1.at[t, q, d])
            else:
                copy = remote(src, dst, t1.at[t, q, d], f1.at[t, q, d], a1, d, 0)
            copy.start()
            lasts[t, q, d] = copy

    def finish(t, q):
        for d in (0, 1, 3, 2):
            lasts[t, q, d].wait()
        total = jnp.zeros((32, BW[t]), F32)
        for s in range(4):
            total = total + vr[t][q, s].astype(F32)
        fin[:, FIN[t, q] : FIN[t, q] + BW[t]] = total.astype(BF)

    for t, q in UNITS:
        expert_rows(t, q)
    for t, q in UNITS:
        combine(t, q)
    for t, q in UNITS:
        narrow(t, q)
    for t, q in UNITS:
        finish(t, q)

    copy = remote(fin.at[block(1 - core, 16), :], outs.at[core], t0.at[0], f0.at[0], "x", 0, 1)
    copy.start()
    outs[core] = fin[block(core, 16), :]
    same = (lax.broadcasted_iota(jnp.int32, (16, 16), 0) == lax.broadcasted_iota(jnp.int32, (16, 16), 1))
    scores = fin[block(core, 16), FIN[1, 0] + 256 : FIN[1, 0] + 384]
    turned = lax.dot_general(scores, same.astype(F32).astype(BF), TN, preferred_element_type=F32)
    gout[...] = turned[0:8].astype(BF)
    copy.wait()
    for half in range(2):
        for unit in UNITS:
            w = BACK_W[unit]
            start = BACK_OFF[unit] + half * w
            out[:, start : start + w] = outs[half, :, FIN[unit] : FIN[unit] + w]


def shards(out_grad, saved_input, routes, gate_int, w_gate, w_up, w_down):
    vmem = pl.BlockSpec(memory_space=pltpu.VMEM)
    hbm = pl.BlockSpec(memory_space=pl.ANY)
    sem = pltpu.SemaphoreType.DMA
    scratch = (
        [pltpu.VMEM((2, 4, 128, w), BF) for w in WIDTHS]
        + [
            pltpu.VMEM((3, 16, 128), F32),
            pltpu.VMEM((3, 8, 16, 128), F32),
            pltpu.VMEM((3, 16, 128), F32),
            pltpu.VMEM((3, 4, 16, 128), F32),
            pltpu.VMEM((3, 2, 256, 256), BF),
            pltpu.VMEM((2, 256, 128), BF),
        ]
        + [pltpu.VMEM((2, 8, 64, w), BF) for w in WIDTHS]
        + [
            pltpu.VMEM((8, 64, 128), F32),
            pltpu.VMEM((256, 128), F32),
            pltpu.VMEM((2, 256, 3584), BF),
            pltpu.VMEM((2, 2, 256, WIDTHS[1]), BF),
            pltpu.VMEM((2, 2, 256, WIDTHS[2]), BF),
            pltpu.VMEM((3584, 1024), BF),
            pltpu.VMEM((3584, 1024), BF),
            pltpu.VMEM((1024, 3584), BF),
            pltpu.VMEM((2, 256, 1024), F32),
            pltpu.VMEM((256, 1024), BF),
            pltpu.VMEM((256, 1024), BF),
            pltpu.VMEM((256, 128), F32),
        ]
        + [pltpu.VMEM((3, 2, 256, w), BF) for w in BW]
        + [pltpu.VMEM((3, 8, 64, w), BF) for w in BW]
        + [pltpu.VMEM((3, 4, 128, w), BF) for w in BW]
        + [pltpu.VMEM((3, 4, 128, w), BF) for w in BW]
        + [pltpu.VMEM((3, 128, w), BF) for w in BW]
        + [pltpu.VMEM((3, 4, 32, w), BF) for w in BW]
        + [
            pltpu.VMEM((32, FIN_W), BF),
            pltpu.VMEM((2, 16, FIN_W), BF),
        ]
        + [
            sem((3,)),
            sem((2, 3, 2)), sem((2, 3)),
            sem((3, 4, 2)), sem((3, 4, 2)),
            sem((2, 3, 4)), sem((2, 3, 4)),
            sem((3, 4)), sem((3, 4)),
            sem((2, 3, 4)), sem((2, 3, 4)),
            sem((2, 3, 4, 2)), sem((2, 3, 4, 2)),
            sem((4,)), sem((4,)),
            sem((2, 3, 4, 2)), sem((2, 3, 4, 2)),
            sem((2, 3, 4)), sem((2, 3, 4)),
            sem((2, 3, 4)), sem((2, 3, 4)),
            sem((1,)), sem((1,)),
        ]
    )
    input_grad, gate_grad = pl.pallas_call(
        kernel,
        out_shape=(
            jax.ShapeDtypeStruct(out_grad.shape, BF),
            jax.ShapeDtypeStruct(routes.shape[::-1], BF),
        ),
        in_specs=[hbm, hbm, vmem, vmem, hbm, hbm, hbm],
        out_specs=(vmem, vmem),
        scratch_shapes=scratch,
        compiler_params=pltpu.CompilerParams(
            collective_id=0, has_side_effects=True, vmem_limit_bytes=64 * 2**20 - 65536
        ),
    )(out_grad, saved_input, routes.T, gate_int.T, w_gate, w_up, w_down)
    return input_grad, gate_grad.T


def solution(mesh):
    rows = P(("node", "local"), None)
    experts = P(("node", "local"), None, None)
    return jax.shard_map(
        shards,
        mesh=mesh,
        in_specs=(rows, rows, rows, rows, experts, experts, experts),
        out_specs=(rows, rows),
        check_vma=False,
    )
```

```python
import functools

import jax
import jax.numpy as jnp
from jax import lax
from jax.experimental import pallas as pl
from jax.experimental.pallas import tpu as pltpu
from jax.sharding import PartitionSpec as P

MESH = pl.DeviceIdType.MESH
BF = jnp.bfloat16
F32 = jnp.float32

ORDERS = (("x", "y", "z"), ("y", "z", "x"), ("z", "x", "y"))
HALF = 1792
WIDTHS = (640, 640, 512)
OFFS = (0, 640, 1280)
UNITS = ((0, 0), (0, 1), (0, 2), (1, 0), (1, 1), (1, 2))
BACK_W = {(0, 0): 256, (0, 1): 256, (0, 2): 256, (1, 0): 256, (1, 1): 384, (1, 2): 384}
BACK_OFF = {(0, 0): 0, (0, 1): 512, (0, 2): 1024, (1, 0): 1536, (1, 1): 2048, (1, 2): 2816}
BW = (256, 384)
STRIDE = {"z": 32, "y": 8, "x": 2}
SPLIT = {"z": 64, "y": 16, "x": 4}
NT = (((1,), (1,)), ((), ()))
TN = (((0,), (0,)), ((), ()))


def coords():
    node = lax.axis_index("node")
    local = lax.axis_index("local")
    return {"z": node // 4, "y": node % 4, "x": local // 2}, local % 2


def native_row(row, order):
    value = {a: (row // SPLIT[a]) % 4 for a in "xyz"}
    a1, a2, a3 = order
    return value[a3] * 64 + value[a2] * 16 + value[a1] * 4 + row % 4


def dot(a, b):
    return jnp.dot(a, b, preferred_element_type=F32)


def kernel(
    og, si, routes, gate_int, wg_hbm, wu_hbm, wd_hbm, out, gout,
    stage, b0, b1, b2, mown, mrecv, msum, ms, smat, kmask, sb0, sb1, sb2, gb, gr, xx, r1, r2,
    wg, wu, wd, pre, gg, gu, score, ysa, ysb, yra, yrb, zsa, zsb, zra, zrb, vsa, vsb, vra, vrb,
    wsem, ssem, snd, msnd, gsnd, rec1, rec2, rec3, rec4, mrec, mrec2, grec, rec5, rec6, rec7,
):
    pos, core = coords()
    bb, sb = (b0, b1, b2), (sb0, sb1, sb2)
    ys, yr, zs, zr, vs, vr = (ysa, ysb), (yra, yrb), (zsa, zsb), (zra, zrb), (vsa, vsb), (vra, vrb)
    KINDS = (1, 0)

    def at(axis, d, cc):
        p = dict(pos)
        p[axis] = (pos[axis] + d) % 4
        return (p["z"] * 4 + p["y"], p["x"] * 2 + (core + cc) % 2)

    def remote(src, dst, send, recv, axis, d, cc):
        return pltpu.make_async_remote_copy(
            src_ref=src, dst_ref=dst, send_sem=send, recv_sem=recv, device_id=at(axis, d, cc), device_id_type=MESH
        )

    def done(view, sem):
        pltpu.make_async_copy(view, view, sem).wait()

    def block(index, size):
        return pl.ds(pl.multiple_of(index * size, size), size)

    loads = [
        pltpu.make_async_copy(hbm.at[0], vmem, wsem.at[i])
        for i, (hbm, vmem) in enumerate(((wg_hbm, wg), (wu_hbm, wu), (wd_hbm, wd)))
    ]
    stages = [pltpu.make_async_copy(ref, stage.at[k], ssem.at[k]) for k, ref in enumerate((og, si))]
    for copy in stages + loads:
        copy.start()

    barrier = pltpu.get_barrier_semaphore()
    partners = [("x", 0, 1)] + [(a, d, cc) for a in "xyz" for d in (1, 2, 3) for cc in (0, 1)]
    for a, d, cc in partners:
        pl.semaphore_signal(barrier, inc=1, device_id=at(a, d, cc), device_id_type=MESH)

    gate_i = gate_int[...]
    table = jnp.concatenate([routes[...], gate_i // 256, gate_i % 256], axis=0).astype(F32).astype(BF)
    token = lax.broadcasted_iota(jnp.int32, (16, 128), 0)
    lane = lax.broadcasted_iota(jnp.int32, (16, 128), 1)
    for q, (a1, a2, a3) in enumerate(ORDERS):
        place = (lane == pos[a1] * 32 + core * 16 + token).astype(F32).astype(BF)
        laid = dot(table, place)
        mown[q, 0:8, :] = laid[0:8]
        mown[q, 8:16, :] = laid[8:16] * 256.0 + laid[16:24]

    for copy in stages:
        copy.wait()
    pl.semaphore_wait(barrier, len(partners))

    hops = [(d, cc) for d in (2, 1, 3, 0) for cc in (1, 0)]
    for k in KINDS:
        for q, (a1, a2, a3) in enumerate(ORDERS):
            dst = bb[q].at[k, pos[a2], block(pos[a1] * 2 + core, 16), :]
            for d, cc in hops:
                half = (core + cc) % 2
                src = stage.at[k, :, pl.ds(pl.multiple_of(half * HALF + OFFS[q], 128), WIDTHS[q])]
                if (d, cc) == (0, 0):
                    pltpu.make_async_copy(src, dst, rec1.at[k, q]).start()
                else:
                    remote(src, dst, snd.at[k, q], rec1.at[k, q], a1, d, cc).start()

    for q, (a1, a2, a3) in enumerate(ORDERS):
        for d, cc in hops:
            if (d, cc) != (0, 0):
                remote(mown.at[q], mrecv.at[q, pos[a1] * 2 + core], msnd.at[q], mrec.at[q], a1, d, cc).start()
        mrecv[q, pos[a1] * 2 + core] = mown[q]

    for k in KINDS:
        for q, (a1, a2, a3) in enumerate(ORDERS):
            done(bb[q].at[k, 0, pl.ds(0, 112), :], snd.at[k, q])
            done(bb[q].at[k, pos[a2]], rec1.at[k, q])
            mine = bb[q].at[k, pos[a2]]
            for d in (1, 3):
                remote(mine, mine, snd.at[k, q], rec2.at[k, q], a2, d, 0).start()

    for q, (a1, a2, a3) in enumerate(ORDERS):
        done(mrecv.at[q, pl.ds(0, 7)], msnd.at[q])
        done(mrecv.at[q, pl.ds(0, 7)], mrec.at[q])
        total = jnp.sum(mrecv[q], axis=0)
        msum[q] = total
        ms[q, pos[a2]] = total
        for d in (2, 1, 3):
            remote(msum.at[q], ms.at[q, pos[a2]], msnd.at[q], mrec2.at[q], a2, d, 0).start()

    for k in KINDS:
        for q, (a1, a2, a3) in enumerate(ORDERS):
            done(bb[q].at[k, pl.ds(0, 2)], snd.at[k, q])
            done(bb[q].at[k, pl.ds(0, 2)], rec2.at[k, q])
            for d, part in ((1, 0), (3, 1)):
                held = bb[q].at[k, (pos[a2] - d) % 4, pl.ds(part * 64, 64), :]
                remote(held, held, snd.at[k, q], rec3.at[k, q], a2, d, 0).start()

    up = lax.broadcasted_iota(jnp.int32, (256, 256), 0)
    across = lax.broadcasted_iota(jnp.int32, (256, 256), 1)
    earlier = ((up < across) & (up // 16 == across // 16)).astype(F32).astype(BF)
    lanes3 = lax.broadcasted_iota(jnp.int32, (8, 32, 128), 2).astype(F32)
    slots3 = lax.broadcasted_iota(jnp.int32, (8, 32, 256), 1).astype(F32)
    picks3 = lax.broadcasted_iota(jnp.int32, (8, 8, 256), 1).astype(F32)
    expert3 = lax.broadcasted_iota(jnp.int32, (8, 8, 256), 0)
    pair = ((lax.broadcasted_iota(jnp.int32, (8, 256), 1) // 16) * 2).astype(F32)

    def tables(q, p):
        a1, a2, a3 = ORDERS[q]
        base = pos[a1] * STRIDE[a1] + pos[a2] * STRIDE[a2]
        expert = ((expert3 // 2) * STRIDE[a3] + expert3 % 2 + base).astype(F32)
        meta = jnp.concatenate([ms[q, 2 * p], ms[q, 2 * p + 1]], axis=1)
        hit = jnp.where(meta[0:8][None] == expert, 1.0, 0.0)
        named = jnp.sum(hit, axis=1)
        rank = dot(named.astype(BF), earlier)
        code = jnp.where(named > 0.5, pair + rank, -1.0)
        chosen = jnp.where(code[:, None, :] == slots3, 1.0, 0.0)
        smat[q, p] = chosen.reshape(256, 256).astype(BF)
        if q == 0:
            gate = jnp.sum(hit * meta[8:16][None], axis=1)
            gate = jnp.sum(chosen * gate[:, None, :], axis=2, keepdims=True)
            gb[:, p * 32 : p * 32 + 32, :] = jnp.broadcast_to(gate * (1.0 / 65536.0), (8, 32, 128))
            pick = jnp.sum(hit * picks3, axis=1)
            pick = jnp.sum(chosen * pick[:, None, :], axis=2, keepdims=True)
            kmask[p] = jnp.where(lanes3 == pick, 1.0, 0.0).reshape(256, 128).astype(BF)

    for q, (a1, a2, a3) in enumerate(ORDERS):
        done(ms.at[q, pl.ds(0, 3)], msnd.at[q])
        done(ms.at[q, pl.ds(0, 3)], mrec2.at[q])
        for p in range(2):
            tables(q, p)

    for k in KINDS:
        for q, (a1, a2, a3) in enumerate(ORDERS):
            done(bb[q].at[k, 0], snd.at[k, q])
            done(bb[q].at[k, 0], rec3.at[k, q])
            for p in range(2):
                rows = dot(smat[q, p], bb[q][k, 2 * p : 2 * p + 2].reshape(256, WIDTHS[q]))
                sb[q][k, :, p * 32 : p * 32 + 32, :] = rows.astype(BF).reshape(8, 32, WIDTHS[q])
            there = block(pos[a3], 64)
            if q == 0:
                land = xx.at[k, there, pl.ds(pl.multiple_of(core * HALF, 128), WIDTHS[0])]
            else:
                land = (r1, r2)[q - 1].at[k, core, there, :]
            for d, cc in hops:
                src = sb[q].at[k, ((pos[a3] + d) % 4) * 2 + (core + cc) % 2]
                if (d, cc) == (0, 0):
                    pltpu.make_async_copy(src, land, rec4.at[k, q]).start()
                else:
                    remote(src, land, snd.at[k, q], rec4.at[k, q], a3, d, cc).start()

    gmine = gr.at[block(pos["z"], 64), :]
    for d in (2, 1, 3, 0):
        src = gb.at[((pos["z"] + d) % 4) * 2 + core]
        if d == 0:
            pltpu.make_async_copy(src, gmine, grec.at[0]).start()
        else:
            remote(src, gmine, gsnd.at[0], grec.at[0], "z", d, 0).start()

    iota_r = lax.broadcasted_iota(jnp.int32, (256, 256), 0)
    iota_c = lax.broadcasted_iota(jnp.int32, (256, 256), 1)

    def arrive(k):
        for q in range(3):
            done(sb[q].at[k, pl.ds(0, 7)], snd.at[k, q])
            done(sb[q].at[k], rec4.at[k, q])
            if q:
                perm = (native_row(iota_r, ORDERS[q]) == iota_c).astype(F32).astype(BF)
                for half in range(2):
                    start = half * HALF + OFFS[q]
                    rows = dot(perm, (r1, r2)[q - 1][k, half])
                    xx[k, :, start : start + WIDTHS[q]] = rows.astype(BF)

    arrive(1)
    for copy in loads:
        copy.wait()

    def forward(n, carry):
        at_n = block(n, 512)
        pre[0, :, at_n] = dot(xx[1], wg[:, at_n])
        pre[1, :, at_n] = dot(xx[1], wu[:, at_n])
        return carry

    lax.fori_loop(0, 2, forward, 0)
    arrive(0)
    score[...] = jnp.zeros_like(score)

    def backward(n, carry):
        at_n = block(n, 512)
        grad_hidden = lax.dot_general(xx[0], wd[at_n, :], NT, preferred_element_type=F32)
        pre_gate = pre[0, :, at_n]
        pre_up = pre[1, :, at_n]
        sig = jax.nn.sigmoid(pre_gate)
        act = pre_gate * sig
        grad_up = grad_hidden * act
        part = grad_up * pre_up
        score[...] += (part[:, 0:128] + part[:, 128:256]) + (part[:, 256:384] + part[:, 384:512])
        gu[:, at_n] = grad_up.astype(BF)
        gg[:, at_n] = (grad_hidden * pre_up * sig * (1.0 + pre_gate * (1.0 - sig))).astype(BF)
        return carry

    lax.fori_loop(0, 2, backward, 0)
    done(gr.at[pl.ds(0, 192), :], gsnd.at[0])
    done(gr, grec.at[0])

    def expert_rows(t, q):
        a1, a2, a3 = ORDERS[q]
        w = BACK_W[t, q]
        cols = pl.ds(BACK_OFF[t, q], 2 * w)
        rows = lax.dot_general(gg[...], wg[cols, :], NT, preferred_element_type=F32)
        rows = rows + lax.dot_general(gu[...], wu[cols, :], NT, preferred_element_type=F32)
        rows = (rows * gr[:, 0:1]).astype(BF)
        if q:
            back = (native_row(iota_c, ORDERS[q]) == iota_r).astype(F32).astype(BF)
            rows = dot(back, rows).astype(BF)
        for half in range(2):
            ys[t][q, half, :, 0:w] = rows[:, half * w : (half + 1) * w]
            if w < BW[t]:
                total = jnp.sum(score[...], axis=1, keepdims=True)
                ys[t][q, half, :, w : BW[t]] = jnp.broadcast_to(total, (256, 128)).astype(BF)
        mine = yr[t].at[q, pos[a3] * 2 + core]
        for d, cc in hops:
            src = ys[t].at[q, (core + cc) % 2, block((pos[a3] + d) % 4, 64), :]
            if (d, cc) == (0, 0):
                pltpu.make_async_copy(src, mine, rec5.at[t, q]).start()
            else:
                remote(src, mine, snd.at[t, q], rec5.at[t, q], a3, d, cc).start()

    def combine(t, q):
        a1, a2, a3 = ORDERS[q]
        done(yr[t].at[q, pl.ds(0, 7)], snd.at[t, q])
        done(yr[t].at[q], rec5.at[t, q])
        for p in range(2):
            got = yr[t][q, :, p * 32 : p * 32 + 32, :].reshape(256, BW[t])
            if BACK_W[t, q] < BW[t]:
                got = jnp.concatenate([got[:, 0:256], got[:, 256:384] * kmask[p]], axis=1)
            total = lax.dot_general(smat[q, p], got, TN, preferred_element_type=F32).astype(BF)
            zs[t][q, 2 * p : 2 * p + 2] = total.reshape(2, 128, BW[t])
        for d in (2, 1, 3, 0):
            src, dst = zs[t].at[q, (pos[a2] + d) % 4], zr[t].at[q, pos[a2]]
            if d == 0:
                pltpu.make_async_copy(src, dst, rec6.at[t, q]).start()
            else:
                remote(src, dst, snd.at[t, q], rec6.at[t, q], a2, d, 0).start()

    def narrow(t, q):
        a1, a2, a3 = ORDERS[q]
        done(zr[t].at[q, pl.ds(0, 3)], snd.at[t, q])
        done(zr[t].at[q], rec6.at[t, q])
        total = jnp.zeros((128, BW[t]), F32)
        for s in range(4):
            total = total + zr[t][q, s].astype(F32)
        vs[t][q] = total.astype(BF)
        dst = vr[t].at[q, core * 4 + pos[a1]]
        for d, cc in hops:
            src = vs[t].at[q, block(((pos[a1] + d) % 4) * 2 + (core + cc) % 2, 16), :]
            if (d, cc) == (0, 0):
                pltpu.make_async_copy(src, dst, rec7.at[t, q]).start()
            else:
                remote(src, dst, snd.at[t, q], rec7.at[t, q], a1, d, cc).start()

    def finish(t, q):
        done(vr[t].at[q, pl.ds(0, 7)], snd.at[t, q])
        done(vr[t].at[q], rec7.at[t, q])
        w = BACK_W[t, q]
        both = jnp.zeros((16, BW[t]), F32)
        for half in range(2):
            total = jnp.zeros((16, BW[t]), F32)
            for s in range(4):
                total = total + vr[t][q, half * 4 + s].astype(F32)
            start = BACK_OFF[t, q] + half * w
            out[:, start : start + w] = total[:, 0:w].astype(BF)
            both = both + total
        if w < BW[t]:
            same = lax.broadcasted_iota(jnp.int32, (16, 16), 0) == lax.broadcasted_iota(jnp.int32, (16, 16), 1)
            scores = (both[:, w : BW[t]] * 0.5).astype(BF)
            turned = lax.dot_general(scores, same.astype(F32).astype(BF), TN, preferred_element_type=F32)
            gout[...] = turned[0:8].astype(BF)

    for t, q in UNITS:
        expert_rows(t, q)
    for t, q in UNITS:
        combine(t, q)
    for t, q in UNITS:
        narrow(t, q)
    for t, q in UNITS:
        finish(t, q)


def shards(out_grad, saved_input, routes, gate_int, w_gate, w_up, w_down):
    vmem = pl.BlockSpec(memory_space=pltpu.VMEM)
    hbm = pl.BlockSpec(memory_space=pl.ANY)
    sem = pltpu.SemaphoreType.DMA
    scratch = (
        [pltpu.VMEM((2, 16, 3584), BF)]
        + [pltpu.VMEM((2, 4, 128, w), BF) for w in WIDTHS]
        + [
            pltpu.VMEM((3, 16, 128), F32),
            pltpu.VMEM((3, 8, 16, 128), F32),
            pltpu.VMEM((3, 16, 128), F32),
            pltpu.VMEM((3, 4, 16, 128), F32),
            pltpu.VMEM((3, 2, 256, 256), BF),
            pltpu.VMEM((2, 256, 128), BF),
        ]
        + [pltpu.VMEM((2, 8, 64, w), BF) for w in WIDTHS]
        + [
            pltpu.VMEM((8, 64, 128), F32),
            pltpu.VMEM((256, 128), F32),
            pltpu.VMEM((2, 256, 3584), BF),
            pltpu.VMEM((2, 2, 256, WIDTHS[1]), BF),
            pltpu.VMEM((2, 2, 256, WIDTHS[2]), BF),
            pltpu.VMEM((3584, 1024), BF),
            pltpu.VMEM((3584, 1024), BF),
            pltpu.VMEM((1024, 3584), BF),
            pltpu.VMEM((2, 256, 1024), F32),
            pltpu.VMEM((256, 1024), BF),
            pltpu.VMEM((256, 1024), BF),
            pltpu.VMEM((256, 128), F32),
        ]
        + [pltpu.VMEM((3, 2, 256, w), BF) for w in BW]
        + [pltpu.VMEM((3, 8, 64, w), BF) for w in BW]
        + [pltpu.VMEM((3, 4, 128, w), BF) for w in BW]
        + [pltpu.VMEM((3, 4, 128, w), BF) for w in BW]
        + [pltpu.VMEM((3, 128, w), BF) for w in BW]
        + [pltpu.VMEM((3, 8, 16, w), BF) for w in BW]
        + [sem((3,)), sem((2,)), sem((2, 3)), sem((3,)), sem((1,))]
        + [sem((2, 3))] * 4
        + [sem((3,)), sem((3,)), sem((1,))]
        + [sem((2, 3))] * 3
    )
    input_grad, gate_grad = pl.pallas_call(
        kernel,
        out_shape=(
            jax.ShapeDtypeStruct(out_grad.shape, BF),
            jax.ShapeDtypeStruct(routes.shape[::-1], BF),
        ),
        in_specs=[hbm, hbm, vmem, vmem, hbm, hbm, hbm],
        out_specs=(vmem, vmem),
        scratch_shapes=scratch,
        compiler_params=pltpu.CompilerParams(
            collective_id=0, has_side_effects=True, vmem_limit_bytes=64 * 2**20 - 65536
        ),
    )(out_grad, saved_input, routes.T, gate_int.T, w_gate, w_up, w_down)
    return input_grad, gate_grad.T


def solution(mesh):
    rows = P(("node", "local"), None)
    experts = P(("node", "local"), None, None)
    return jax.shard_map(
        shards,
        mesh=mesh,
        in_specs=(rows, rows, rows, rows, experts, experts, experts),
        out_specs=(rows, rows),
        check_vma=False,
    )
```

```python
import functools

import jax
import jax.numpy as jnp
from jax import lax
from jax.experimental import pallas as pl
from jax.experimental.pallas import tpu as pltpu
from jax.sharding import PartitionSpec as P

MESH = pl.DeviceIdType.MESH
BF = jnp.bfloat16
F32 = jnp.float32

ORDERS = (("x", "y", "z"), ("y", "z", "x"), ("z", "x", "y"))
HALF = 1792
WIDTHS = (640, 640, 512)
OFFS = (0, 640, 1280)
UNITS = ((0, 0), (0, 1), (0, 2), (1, 0), (1, 1), (1, 2))
BACK_W = {(0, 0): 256, (0, 1): 256, (0, 2): 256, (1, 0): 256, (1, 1): 384, (1, 2): 384}
BACK_OFF = {(0, 0): 0, (0, 1): 512, (0, 2): 1024, (1, 0): 1536, (1, 1): 2048, (1, 2): 2816}
BW = (256, 384)
STRIDE = {"z": 32, "y": 8, "x": 2}
SPLIT = {"z": 64, "y": 16, "x": 4}
NT = (((1,), (1,)), ((), ()))
TN = (((0,), (0,)), ((), ()))


def coords():
    node = lax.axis_index("node")
    local = lax.axis_index("local")
    return {"z": node // 4, "y": node % 4, "x": local // 2}, local % 2


def native_row(row, order):
    value = {a: (row // SPLIT[a]) % 4 for a in "xyz"}
    a1, a2, a3 = order
    return value[a3] * 64 + value[a2] * 16 + value[a1] * 4 + row % 4


def dot(a, b):
    return jnp.dot(a, b, preferred_element_type=F32)


def kernel(
    og, si, routes, gate_int, wg_hbm, wu_hbm, wd_hbm, out, gout,
    stage, b0, b1, b2, mown, mrecv, msum, ms, smat, turn, order, kmask, sb0, sb1, sb2, gb, gr, xx, r1, r2,
    wg, wu, wd, pre, gg, gu, score, ysa, ysb, yra, yrb, zsa, zsb, zra, zrb, vsa, vsb, vra, vrb,
    wsem, ssem, snd, msnd, gsnd, rec1, rec2, rec3, rec4, mrec, mrec2, grec, rec5, rec6, rec7,
):
    pos, core = coords()
    bb, sb = (b0, b1, b2), (sb0, sb1, sb2)
    ys, yr, zs, zr, vs, vr = (ysa, ysb), (yra, yrb), (zsa, zsb), (zra, zrb), (vsa, vsb), (vra, vrb)
    KINDS = (1, 0)

    def at(axis, d, cc):
        p = dict(pos)
        p[axis] = (pos[axis] + d) % 4
        return (p["z"] * 4 + p["y"], p["x"] * 2 + (core + cc) % 2)

    def remote(src, dst, send, recv, axis, d, cc):
        return pltpu.make_async_remote_copy(
            src_ref=src, dst_ref=dst, send_sem=send, recv_sem=recv, device_id=at(axis, d, cc), device_id_type=MESH
        )

    def done(view, sem):
        pltpu.make_async_copy(view, view, sem).wait()

    def block(index, size):
        return pl.ds(pl.multiple_of(index * size, size), size)

    loads = [
        pltpu.make_async_copy(hbm.at[0], vmem, wsem.at[i])
        for i, (hbm, vmem) in enumerate(((wg_hbm, wg), (wu_hbm, wu), (wd_hbm, wd)))
    ]
    stages = [pltpu.make_async_copy(ref, stage.at[k], ssem.at[k]) for k, ref in enumerate((og, si))]
    for copy in stages:
        copy.start()

    barrier = pltpu.get_barrier_semaphore()
    partners = [("x", 0, 1)] + [(a, d, cc) for a in "xyz" for d in (1, 2, 3) for cc in (0, 1)]
    for a, d, cc in partners:
        pl.semaphore_signal(barrier, inc=1, device_id=at(a, d, cc), device_id_type=MESH)

    gate_i = gate_int[...]
    table = jnp.concatenate([routes[...], gate_i // 256, gate_i % 256], axis=0).astype(F32).astype(BF)
    token = lax.broadcasted_iota(jnp.int32, (16, 128), 0)
    lane = lax.broadcasted_iota(jnp.int32, (16, 128), 1)
    for q, (a1, a2, a3) in enumerate(ORDERS):
        place = (lane == pos[a1] * 32 + core * 16 + token).astype(F32).astype(BF)
        laid = dot(table, place)
        mown[q, 0:8, :] = laid[0:8]
        mown[q, 8:16, :] = laid[8:16] * 256.0 + laid[16:24]

    iota_r = lax.broadcasted_iota(jnp.int32, (256, 256), 0)
    iota_c = lax.broadcasted_iota(jnp.int32, (256, 256), 1)
    for q in (1, 2):
        order[q - 1, 0] = (native_row(iota_r, ORDERS[q]) == iota_c).astype(F32).astype(BF)
        order[q - 1, 1] = (native_row(iota_c, ORDERS[q]) == iota_r).astype(F32).astype(BF)

    for copy in stages:
        copy.wait()
    pl.semaphore_wait(barrier, len(partners))

    hops = [(d, cc) for d in (2, 1, 3, 0) for cc in (1, 0)]
    for k in KINDS:
        for q, (a1, a2, a3) in enumerate(ORDERS):
            dst = bb[q].at[k, pos[a2], block(pos[a1] * 2 + core, 16), :]
            for d, cc in hops:
                half = (core + cc) % 2
                src = stage.at[k, :, pl.ds(pl.multiple_of(half * HALF + OFFS[q], 128), WIDTHS[q])]
                if (d, cc) == (0, 0):
                    pltpu.make_async_copy(src, dst, rec1.at[k, q]).start()
                else:
                    remote(src, dst, snd.at[k, q], rec1.at[k, q], a1, d, cc).start()

    for q, (a1, a2, a3) in enumerate(ORDERS):
        for d, cc in hops:
            if (d, cc) != (0, 0):
                remote(mown.at[q], mrecv.at[q, pos[a1] * 2 + core], msnd.at[q], mrec.at[q], a1, d, cc).start()
        mrecv[q, pos[a1] * 2 + core] = mown[q]

    for k in KINDS:
        for q, (a1, a2, a3) in enumerate(ORDERS):
            done(bb[q].at[k, 0, pl.ds(0, 112), :], snd.at[k, q])
            done(bb[q].at[k, pos[a2]], rec1.at[k, q])
            mine = bb[q].at[k, pos[a2]]
            for d in (1, 3):
                remote(mine, mine, snd.at[k, q], rec2.at[k, q], a2, d, 0).start()

    for copy in loads:
        copy.start()

    for q, (a1, a2, a3) in enumerate(ORDERS):
        done(mrecv.at[q, pl.ds(0, 7)], msnd.at[q])
        done(mrecv.at[q, pl.ds(0, 7)], mrec.at[q])
        total = jnp.sum(mrecv[q], axis=0)
        msum[q] = total
        ms[q, pos[a2]] = total
        for d in (2, 1, 3):
            remote(msum.at[q], ms.at[q, pos[a2]], msnd.at[q], mrec2.at[q], a2, d, 0).start()

    for k in KINDS:
        for q, (a1, a2, a3) in enumerate(ORDERS):
            done(bb[q].at[k, pl.ds(0, 2)], snd.at[k, q])
            done(bb[q].at[k, pl.ds(0, 2)], rec2.at[k, q])
            for d, part in ((1, 0), (3, 1)):
                held = bb[q].at[k, (pos[a2] - d) % 4, pl.ds(part * 64, 64), :]
                remote(held, held, snd.at[k, q], rec3.at[k, q], a2, d, 0).start()

    up = lax.broadcasted_iota(jnp.int32, (256, 256), 0)
    across = lax.broadcasted_iota(jnp.int32, (256, 256), 1)
    earlier = ((up < across) & (up // 16 == across // 16)).astype(F32).astype(BF)
    lanes3 = lax.broadcasted_iota(jnp.int32, (8, 32, 128), 2).astype(F32)
    slots3 = lax.broadcasted_iota(jnp.int32, (8, 32, 256), 1).astype(F32)
    picks3 = lax.broadcasted_iota(jnp.int32, (8, 8, 256), 1).astype(F32)
    expert3 = lax.broadcasted_iota(jnp.int32, (8, 8, 256), 0)
    pair = ((lax.broadcasted_iota(jnp.int32, (8, 256), 1) // 16) * 2).astype(F32)

    def tables(q, p):
        a1, a2, a3 = ORDERS[q]
        base = pos[a1] * STRIDE[a1] + pos[a2] * STRIDE[a2]
        expert = ((expert3 // 2) * STRIDE[a3] + expert3 % 2 + base).astype(F32)
        meta = jnp.concatenate([ms[q, 2 * p], ms[q, 2 * p + 1]], axis=1)
        hit = jnp.where(meta[0:8][None] == expert, 1.0, 0.0)
        named = jnp.sum(hit, axis=1)
        rank = dot(named.astype(BF), earlier)
        code = jnp.where(named > 0.5, pair + rank, -1.0)
        chosen = jnp.where(code[:, None, :] == slots3, 1.0, 0.0)
        chosen2 = chosen.reshape(256, 256)
        smat[q, p] = chosen2.astype(BF)
        turn[q, p] = chosen2.T.astype(BF)
        if q == 0:
            gate = jnp.sum(hit * meta[8:16][None], axis=1)
            gate = jnp.sum(chosen * gate[:, None, :], axis=2, keepdims=True)
            gb[:, p * 32 : p * 32 + 32, :] = jnp.broadcast_to(gate * (1.0 / 65536.0), (8, 32, 128))
            pick = jnp.sum(hit * picks3, axis=1)
            pick = jnp.sum(chosen * pick[:, None, :], axis=2, keepdims=True)
            kmask[p] = jnp.where(lanes3 == pick, 1.0, 0.0).reshape(256, 128).astype(BF)

    for q, (a1, a2, a3) in enumerate(ORDERS):
        done(ms.at[q, pl.ds(0, 3)], msnd.at[q])
        done(ms.at[q, pl.ds(0, 3)], mrec2.at[q])
        for p in range(2):
            tables(q, p)

    for k in KINDS:
        for q, (a1, a2, a3) in enumerate(ORDERS):
            done(bb[q].at[k, 0], snd.at[k, q])
            done(bb[q].at[k, 0], rec3.at[k, q])
            for p in range(2):
                rows = dot(smat[q, p], bb[q][k, 2 * p : 2 * p + 2].reshape(256, WIDTHS[q]))
                sb[q][k, :, p * 32 : p * 32 + 32, :] = rows.astype(BF).reshape(8, 32, WIDTHS[q])
            there = block(pos[a3], 64)
            if q == 0:
                land = xx.at[k, there, pl.ds(pl.multiple_of(core * HALF, 128), WIDTHS[0])]
            else:
                land = (r1, r2)[q - 1].at[k, core, there, :]
            for d, cc in hops:
                src = sb[q].at[k, ((pos[a3] + d) % 4) * 2 + (core + cc) % 2]
                if (d, cc) == (0, 0):
                    pltpu.make_async_copy(src, land, rec4.at[k, q]).start()
                else:
                    remote(src, land, snd.at[k, q], rec4.at[k, q], a3, d, cc).start()

    gmine = gr.at[block(pos["z"], 64), :]
    for d in (2, 1, 3, 0):
        src = gb.at[((pos["z"] + d) % 4) * 2 + core]
        if d == 0:
            pltpu.make_async_copy(src, gmine, grec.at[0]).start()
        else:
            remote(src, gmine, gsnd.at[0], grec.at[0], "z", d, 0).start()

    def arrive(k):
        for q in range(3):
            done(sb[q].at[k, pl.ds(0, 7)], snd.at[k, q])
            done(sb[q].at[k], rec4.at[k, q])
            if q:
                for half in range(2):
                    start = half * HALF + OFFS[q]
                    rows = dot(order[q - 1, 0], (r1, r2)[q - 1][k, half])
                    xx[k, :, start : start + WIDTHS[q]] = rows.astype(BF)

    arrive(1)
    for copy in loads:
        copy.wait()

    def forward(n, carry):
        at_n = block(n, 512)
        pre[0, :, at_n] = dot(xx[1], wg[:, at_n])
        pre[1, :, at_n] = dot(xx[1], wu[:, at_n])
        return carry

    lax.fori_loop(0, 2, forward, 0)
    arrive(0)
    score[...] = jnp.zeros_like(score)

    def backward(n, carry):
        at_n = block(n, 512)
        grad_hidden = lax.dot_general(xx[0], wd[at_n, :], NT, preferred_element_type=F32)
        pre_gate = pre[0, :, at_n]
        pre_up = pre[1, :, at_n]
        sig = jax.nn.sigmoid(pre_gate)
        act = pre_gate * sig
        grad_up = grad_hidden * act
        part = grad_up * pre_up
        score[...] += (part[:, 0:128] + part[:, 128:256]) + (part[:, 256:384] + part[:, 384:512])
        gu[:, at_n] = grad_up.astype(BF)
        gg[:, at_n] = (grad_hidden * pre_up * sig * (1.0 + pre_gate * (1.0 - sig))).astype(BF)
        return carry

    lax.fori_loop(0, 2, backward, 0)
    done(gr.at[pl.ds(0, 192), :], gsnd.at[0])
    done(gr, grec.at[0])

    def expert_rows(t, q):
        a1, a2, a3 = ORDERS[q]
        w = BACK_W[t, q]
        cols = pl.ds(BACK_OFF[t, q], 2 * w)
        rows = lax.dot_general(gg[...], wg[cols, :], NT, preferred_element_type=F32)
        rows = rows + lax.dot_general(gu[...], wu[cols, :], NT, preferred_element_type=F32)
        rows = (rows * gr[:, 0:1]).astype(BF)
        if q:
            rows = dot(order[q - 1, 1], rows).astype(BF)
        for half in range(2):
            ys[t][q, half, :, 0:w] = rows[:, half * w : (half + 1) * w]
            if w < BW[t]:
                total = jnp.sum(score[...], axis=1, keepdims=True)
                ys[t][q, half, :, w : BW[t]] = jnp.broadcast_to(total, (256, 128)).astype(BF)
        mine = yr[t].at[q, pos[a3] * 2 + core]
        for d, cc in hops:
            src = ys[t].at[q, (core + cc) % 2, block((pos[a3] + d) % 4, 64), :]
            if (d, cc) == (0, 0):
                pltpu.make_async_copy(src, mine, rec5.at[t, q]).start()
            else:
                remote(src, mine, snd.at[t, q], rec5.at[t, q], a3, d, cc).start()

    def combine(t, q):
        a1, a2, a3 = ORDERS[q]
        done(yr[t].at[q, pl.ds(0, 7)], snd.at[t, q])
        done(yr[t].at[q], rec5.at[t, q])
        for p in range(2):
            got = yr[t][q, :, p * 32 : p * 32 + 32, :].reshape(256, BW[t])
            if BACK_W[t, q] < BW[t]:
                got = jnp.concatenate([got[:, 0:256], got[:, 256:384] * kmask[p]], axis=1)
            total = dot(turn[q, p], got).astype(BF)
            zs[t][q, 2 * p : 2 * p + 2] = total.reshape(2, 128, BW[t])
        for d in (2, 1, 3, 0):
            src, dst = zs[t].at[q, (pos[a2] + d) % 4], zr[t].at[q, pos[a2]]
            if d == 0:
                pltpu.make_async_copy(src, dst, rec6.at[t, q]).start()
            else:
                remote(src, dst, snd.at[t, q], rec6.at[t, q], a2, d, 0).start()

    def narrow(t, q):
        a1, a2, a3 = ORDERS[q]
        done(zr[t].at[q, pl.ds(0, 3)], snd.at[t, q])
        done(zr[t].at[q], rec6.at[t, q])
        total = jnp.zeros((128, BW[t]), F32)
        for s in range(4):
            total = total + zr[t][q, s].astype(F32)
        vs[t][q] = total.astype(BF)
        dst = vr[t].at[q, core * 4 + pos[a1]]
        for d, cc in hops:
            src = vs[t].at[q, block(((pos[a1] + d) % 4) * 2 + (core + cc) % 2, 16), :]
            if (d, cc) == (0, 0):
                pltpu.make_async_copy(src, dst, rec7.at[t, q]).start()
            else:
                remote(src, dst, snd.at[t, q], rec7.at[t, q], a1, d, cc).start()

    def finish(t, q):
        done(vr[t].at[q, pl.ds(0, 7)], snd.at[t, q])
        done(vr[t].at[q], rec7.at[t, q])
        w = BACK_W[t, q]
        both = jnp.zeros((16, BW[t]), F32)
        for half in range(2):
            total = jnp.zeros((16, BW[t]), F32)
            for s in range(4):
                total = total + vr[t][q, half * 4 + s].astype(F32)
            start = BACK_OFF[t, q] + half * w
            out[:, start : start + w] = total[:, 0:w].astype(BF)
            both = both + total
        if w < BW[t]:
            same = lax.broadcasted_iota(jnp.int32, (16, 16), 0) == lax.broadcasted_iota(jnp.int32, (16, 16), 1)
            scores = (both[:, w : BW[t]] * 0.5).astype(BF)
            turned = lax.dot_general(scores, same.astype(F32).astype(BF), TN, preferred_element_type=F32)
            gout[...] = turned[0:8].astype(BF)

    for t, q in UNITS:
        expert_rows(t, q)
    for t, q in UNITS:
        combine(t, q)
    for t, q in UNITS:
        narrow(t, q)
    for t, q in UNITS:
        finish(t, q)


def hand_over(rows, scores, out, gout):
    out[...] = rows[...]
    gout[...] = scores[...]


def shards(out_grad, saved_input, routes, gate_int, w_gate, w_up, w_down):
    vmem = pl.BlockSpec(memory_space=pltpu.VMEM)
    hbm = pl.BlockSpec(memory_space=pl.ANY)
    sem = pltpu.SemaphoreType.DMA
    scratch = (
        [pltpu.VMEM((2, 16, 3584), BF)]
        + [pltpu.VMEM((2, 4, 128, w), BF) for w in WIDTHS]
        + [
            pltpu.VMEM((3, 16, 128), F32),
            pltpu.VMEM((3, 8, 16, 128), F32),
            pltpu.VMEM((3, 16, 128), F32),
            pltpu.VMEM((3, 4, 16, 128), F32),
            pltpu.VMEM((3, 2, 256, 256), BF),
            pltpu.VMEM((3, 2, 256, 256), BF),
            pltpu.VMEM((2, 2, 256, 256), BF),
            pltpu.VMEM((2, 256, 128), BF),
        ]
        + [pltpu.VMEM((2, 8, 64, w), BF) for w in WIDTHS]
        + [
            pltpu.VMEM((8, 64, 128), F32),
            pltpu.VMEM((256, 128), F32),
            pltpu.VMEM((2, 256, 3584), BF),
            pltpu.VMEM((2, 2, 256, WIDTHS[1]), BF),
            pltpu.VMEM((2, 2, 256, WIDTHS[2]), BF),
            pltpu.VMEM((3584, 1024), BF),
            pltpu.VMEM((3584, 1024), BF),
            pltpu.VMEM((1024, 3584), BF),
            pltpu.VMEM((2, 256, 1024), F32),
            pltpu.VMEM((256, 1024), BF),
            pltpu.VMEM((256, 1024), BF),
            pltpu.VMEM((256, 128), F32),
        ]
        + [pltpu.VMEM((3, 2, 256, w), BF) for w in BW]
        + [pltpu.VMEM((3, 8, 64, w), BF) for w in BW]
        + [pltpu.VMEM((3, 4, 128, w), BF) for w in BW]
        + [pltpu.VMEM((3, 4, 128, w), BF) for w in BW]
        + [pltpu.VMEM((3, 128, w), BF) for w in BW]
        + [pltpu.VMEM((3, 8, 16, w), BF) for w in BW]
        + [sem((3,)), sem((2,)), sem((2, 3)), sem((3,)), sem((1,))]
        + [sem((2, 3))] * 4
        + [sem((3,)), sem((3,)), sem((1,))]
        + [sem((2, 3))] * 3
    )
    input_grad, gate_grad = pl.pallas_call(
        kernel,
        out_shape=(
            jax.ShapeDtypeStruct(out_grad.shape, BF),
            jax.ShapeDtypeStruct(routes.shape[::-1], BF),
        ),
        in_specs=[hbm, hbm, vmem, vmem, hbm, hbm, hbm],
        out_specs=(vmem, vmem),
        scratch_shapes=scratch,
        compiler_params=pltpu.CompilerParams(
            collective_id=0, has_side_effects=True, vmem_limit_bytes=64 * 2**20 - 65536
        ),
    )(out_grad, saved_input, routes.T, gate_int.T, w_gate, w_up, w_down)
    input_grad, gate_grad = pl.pallas_call(
        hand_over,
        out_shape=(
            jax.ShapeDtypeStruct(out_grad.shape, BF),
            jax.ShapeDtypeStruct(routes.shape[::-1], BF),
        ),
        in_specs=[vmem, vmem],
        out_specs=(vmem, vmem),
    )(input_grad, gate_grad)
    return input_grad, gate_grad.T


def solution(mesh):
    rows = P(("node", "local"), None)
    experts = P(("node", "local"), None, None)
    return jax.shard_map(
        shards,
        mesh=mesh,
        in_specs=(rows, rows, rows, rows, experts, experts, experts),
        out_specs=(rows, rows),
        check_vma=False,
    )
```
